32 devices in a mesh: ctx: 8 (over z, y), head: 4 (over x, core).
Axes of the slice: x: 2, y: 2, z: 4, core: 2. Of those that a mesh axis runs over, the one named last changes fastest.
Arguments:
- query: bfloat16 [8, 64, 576], P('ctx', 'head'), may hold values from -20 to 20
- cache: bfloat16 [32768, 576], P('ctx'), may hold values from -20 to 20
- cotangent: bfloat16 [8, 64, 512], P('ctx', 'head'), may hold values from -6 to 6
- positions: int32 [8], P('ctx'), may hold values from 0 to 262143
- visible: int32 [8], replicated, may hold values from 128 to 32768, as said below
Outputs:
- attention: bfloat16 [8, 64, 512], P('ctx', 'head')
- grad_query: float32 [8, 64, 576], P('ctx', 'head')
- grad_cache: bfloat16 [32768, 576], P('ctx')
The draws below stay inside these ranges and needn't reach their ends.
Inputs may be any that keep to these rules, and one draw needn't show every extreme that they name: `visible`: each entry is a multiple of 128; some rollout token sees all 32768 prompt tokens.
All inputs are finite; a program needn't handle non-finite values.
Results may differ from the reference program's by a relative error of at most 0.01855.
Values may be sent and summed in bfloat16 or wider, within the bound.
No kernel may reach another device: no remote copies, remote signals or barrier semaphores. Data moves between devices by JAX's collectives and lax.ppermute only.
A program may use at most 128 MiB of HBM per device.

```python
import jax
import jax.numpy as jnp
import numpy as np
from jax import lax

VDIM = 512
RDIM = 64
BLOCK = 128
HEADS = 64
TOKENS = 8
PROMPT = 32768


def planted_row(key):
    amplitude = (160.0 * 192.0 ** 0.5 / VDIM) ** 0.5
    sign_bits = jax.random.bernoulli(jax.random.fold_in(key, 91), 0.5, (VDIM,))
    return jnp.where(sign_bits, amplitude, -amplitude).astype(jnp.float32)


def draw_query(key, part):
    full_shape = (TOKENS, HEADS, VDIM + RDIM)
    drawn = jnp.clip(jax.random.normal(jax.random.fold_in(key, 1), full_shape), -4.0, 4.0)
    planted = planted_row(key)
    padding = jnp.zeros((RDIM,), jnp.float32)
    strengths = [0.7, 1.0, 1.5]
    head_slots = [0, HEADS // 2, HEADS - 1]
    for slot_index in range(3):
        planted_query = jnp.concatenate([strengths[slot_index] * planted, padding])
        drawn = drawn.at[slot_index, head_slots[slot_index]].set(planted_query)
    return drawn.astype(jnp.bfloat16)


def draw_cache(key, part):
    full_shape = (PROMPT, VDIM + RDIM)
    drawn = jnp.clip(jax.random.normal(jax.random.fold_in(key, 3), full_shape), -4.0, 4.0)
    planted = planted_row(key)
    alternate = jnp.where(jnp.arange(VDIM) % 2 == 0, 0.5, -0.5)
    second = planted * (0.9875 + alternate)
    padding = jnp.zeros((RDIM,), jnp.float32)
    drawn = drawn.at[0].set(jnp.concatenate([planted, padding]))
    drawn = drawn.at[1].set(jnp.concatenate([second, padding]))
    return drawn.astype(jnp.bfloat16)


def draw_visible(key, part):
    blocks = PROMPT // BLOCK
    counts = jax.random.randint(jax.random.fold_in(key, 5), (TOKENS,), 1, blocks + 1)
    chosen = jax.random.randint(jax.random.fold_in(key, 6), (), 0, TOKENS)
    counts = jnp.where(jnp.arange(TOKENS) == chosen, blocks, counts)
    return (counts * BLOCK).astype(jnp.int32)


def place_ends(values, own_key, low, top_value):
    shape = values.shape
    index_at = [jax.random.randint(jax.random.fold_in(own_key, axis), (), 0, shape[axis]) for axis in range(len(shape))]
    values = values.at[tuple(index_at)].set(low)
    longest = shape.index(max(shape))
    index_at[longest] = (index_at[longest] + 1) % shape[longest]
    return values.at[tuple(index_at)].set(top_value)


def levels(stream_key, shape, cuts, low, high):
    loudness, own = 1.0, jax.random.fold_in(stream_key, 6)
    for position, blocks in cuts:
        heights = jnp.exp(jax.random.uniform(jax.random.fold_in(own, position), (blocks,), jnp.float32, low / len(cuts), high / len(cuts)))
        loudness = loudness * jnp.repeat(heights, shape[position] // blocks).reshape([-1 if axis == position else 1 for axis in range(len(shape))])
    return loudness


def normal_values(own_key, dims, width, most, split=(), held_as=jnp.bfloat16):
    gain = levels(own_key, dims, split, -0.22, 0.18) if split else 1.0
    values = jax.random.normal(own_key, dims, jnp.float32) * width * gain
    return jnp.minimum(jnp.maximum(values, -most), most).astype(held_as)


def setup_inputs(seed: int = 0) -> dict:
    keys = jax.random.split(jax.random.key(seed), 6)
    return {
        "query": draw_query(jax.random.fold_in(keys[5], 71), 0),
        "cache": draw_cache(jax.random.fold_in(keys[5], 71), 0),
        "cotangent": normal_values(keys[2], (TOKENS, HEADS, VDIM), 1.0, 6.0, ((0, 8), (1, 4))),
        "positions": place_ends(jax.random.randint(keys[3], (TOKENS,), 0, 262144), jax.random.fold_in(keys[3], 1), 0, 262143).astype(jnp.int32),
        "visible": draw_visible(jax.random.fold_in(keys[5], 71), 0),
    }


softmax_scale = 192.0 ** -0.5
position_bits = 18
masked_value = -1.0e30


def rotation(positions, half_width):
    frequency = 10000.0 ** (-np.arange(half_width) / half_width)
    angles = np.outer(2.0 ** np.arange(position_bits), frequency)
    cosine_table = jnp.asarray(np.cos(angles), jnp.float32)
    sine_table = jnp.asarray(np.sin(angles), jnp.float32)
    cosines = jnp.ones((positions.shape[0], half_width), jnp.float32)
    sine_part = jnp.zeros((positions.shape[0], half_width), jnp.float32)
    for bit_index in range(position_bits):
        switch = ((positions // (2 ** bit_index)) % 2).astype(jnp.float32)[:, None]
        step_cos = 1.0 + switch * (cosine_table[bit_index] - 1.0)
        step_sin = switch * sine_table[bit_index]
        cosines, sine_part = cosines * step_cos - sine_part * step_sin, sine_part * step_cos + cosines * step_sin
    return cosines[:, None, :], sine_part[:, None, :]


def rotate(tensor, cosines, sine_part, value_width, inverse):
    half_width = cosines.shape[-1]
    lower = tensor[..., value_width:value_width + half_width]
    upper = tensor[..., value_width + half_width:]
    if inverse:
        sine_part = -sine_part
    new_lower = lower * cosines - upper * sine_part
    new_upper = lower * sine_part + upper * cosines
    return jnp.concatenate([tensor[..., :value_width], new_lower, new_upper], axis=-1)


def reference(query, cache, cotangent, positions, visible):
    value_width = cotangent.shape[-1]
    half_width = (query.shape[-1] - value_width) // 2
    cosines, sine_part = rotation(positions, half_width)
    rotated = rotate(query.astype(jnp.float32), cosines, sine_part, value_width, False).astype(jnp.bfloat16)
    allowed = jnp.arange(cache.shape[0]).astype(jnp.int32)[None, :] < visible[:, None]
    values = cache[:, :value_width]
    extra_width = cache.shape[1] - value_width

    def per_head(carry, inputs):
        query_head, grad_head = inputs
        scores = jnp.dot(query_head, cache.T, preferred_element_type=jnp.float32) * softmax_scale
        scores = jnp.where(allowed, scores, masked_value)
        peak = jnp.max(scores, axis=1, keepdims=True)
        weights = jnp.where(allowed, jnp.exp(scores - peak), 0.0)
        totals = jnp.sum(weights, axis=1, keepdims=True)
        probs = weights / totals
        prob_low = probs.astype(jnp.bfloat16)
        attended = jnp.dot(prob_low, values, preferred_element_type=jnp.float32)
        grad_probs = jnp.dot(grad_head, values.T, preferred_element_type=jnp.float32)
        delta = jnp.sum(grad_head.astype(jnp.float32) * attended, axis=1, keepdims=True)
        grad_scores = (probs * (grad_probs - delta) * softmax_scale).astype(jnp.bfloat16)
        grad_rotated = jnp.dot(grad_scores, cache, preferred_element_type=jnp.float32)
        grad_latent = jnp.dot(grad_scores.T, query_head, preferred_element_type=jnp.float32)
        grad_value = jnp.dot(prob_low.T, grad_head, preferred_element_type=jnp.float32)
        grad_latent = grad_latent + jnp.pad(grad_value, ((0, 0), (0, extra_width)))
        return carry + grad_latent, (attended, grad_rotated)

    start = jnp.zeros(cache.shape, jnp.float32)
    summed, (attended, grad_rotated) = lax.scan(per_head, start, (jnp.swapaxes(rotated, 0, 1), jnp.swapaxes(cotangent, 0, 1)))
    attention = jnp.swapaxes(attended, 0, 1).astype(jnp.bfloat16)
    grad_query = rotate(jnp.swapaxes(grad_rotated, 0, 1), cosines, sine_part, value_width, True)
    return attention, grad_query, summed.astype(jnp.bfloat16)
```

```python
import functools

import jax
import jax.numpy as jnp
import numpy as np
from jax import lax
from jax.experimental import pallas as pl
from jax.experimental.pallas import tpu as pltpu
from jax.sharding import PartitionSpec as P

softmax_scale = 192.0 ** (-0.5)
exp2_scale = softmax_scale * float(np.log2(np.e))
position_bits = 18
masked_value = -1e30
peak_floor = -1e29

MINOR = (((1,), (1,)), ((), ()))
MAJOR = (((1,), (0,)), ((), ()))


def matmul(a, b, dims):
    return lax.dot_general(a, b, dims, preferred_element_type=jnp.float32)


def rotation_tables(half_width):
    frequency = 10000.0 ** (-np.arange(half_width) / half_width)
    angles = np.outer(2.0 ** np.arange(position_bits), frequency)
    cosine = np.cos(angles).astype(np.float32)
    sine = np.sin(angles).astype(np.float32)
    return np.concatenate([cosine, cosine], 1), np.concatenate([-sine, sine], 1)


def swap_matrix(half_width):
    return np.roll(np.eye(2 * half_width, dtype=np.float32), half_width, 0)


def prepare_kernel(position_ref, query_ref, cotangent_ref, cos_ref, sin_ref, swap_ref, packed_ref, turn_ref):
    tokens, heads, width = query_ref.shape
    values = cotangent_ref.shape[2]
    rotary = width - values
    swap = swap_ref[...].astype(jnp.bfloat16)
    for t in range(tokens):
        position = position_ref[t]
        cosine = jnp.ones((1, rotary), jnp.float32)
        sine = jnp.zeros((1, rotary), jnp.float32)
        for bit in range(position_bits):
            switch = (lax.shift_right_logical(position, bit) & 1).astype(jnp.float32)
            step_cos = 1.0 + switch * (cos_ref[bit : bit + 1, :] - 1.0)
            step_sin = switch * sin_ref[bit : bit + 1, :]
            cosine, sine = cosine * step_cos - sine * step_sin, sine * step_cos + cosine * step_sin
        turn_ref[t, 0:1, :] = cosine
        turn_ref[t, 1:2, :] = sine
        rope = query_ref[t, :, values:]
        turned = rope.astype(jnp.float32) * cosine + matmul(rope, swap, MAJOR) * sine
        for c in range(packed_ref.shape[0]):
            packed_ref[c, t, :, :values] = cotangent_ref[t]
            packed_ref[c, t, :, values : 2 * values] = query_ref[t, :, :values]
            packed_ref[c, t, :, 2 * values :] = turned.astype(jnp.bfloat16)


def score_kernel(chunks, heads, first_ref, visible_ref, packed_ref, cache_ref, weights_ref, stats_ref, cache_buf, scores, grads, sems):
    rows = packed_ref.shape[0]
    keys, width = cache_ref.shape
    values = packed_ref.shape[1] - width
    tokens = rows // heads
    size = keys // chunks

    def fetch(c):
        part = pl.ds(c * size, size)
        return pltpu.make_async_copy(cache_ref.at[part], cache_buf.at[part], sems.at[c])

    for c in range(chunks):
        fetch(c).start()
    token_of = lax.broadcasted_iota(jnp.int32, (rows, 1), 0) // heads
    limit = jnp.zeros((rows, 1), jnp.int32)
    for t in range(tokens):
        limit = jnp.where(token_of == t, visible_ref[t], limit)
    limit = limit - first_ref[0]
    cotangent = packed_ref[:, :values]
    rotated = packed_ref[:, values:]
    peak = jnp.full((rows, 128), peak_floor, jnp.float32)
    lane = lax.broadcasted_iota(jnp.int32, (rows, size), 1)
    for c in range(chunks):
        fetch(c).wait()
        block = cache_buf[c * size : (c + 1) * size, :]
        score = matmul(rotated, block, MINOR) * exp2_scale
        score = jnp.where(lane < limit - c * size, score, masked_value)
        scores[:, c * size : (c + 1) * size] = score
        for i in range(size // 128):
            peak = jnp.maximum(peak, score[:, i * 128 : (i + 1) * 128])
        grads[:, c * size : (c + 1) * size] = matmul(cotangent, block[:, :values], MINOR)
    peak = jnp.max(peak, axis=1, keepdims=True)
    mass = jnp.zeros((rows, 128), jnp.float32)
    moment = jnp.zeros((rows, 128), jnp.float32)
    for i in range(keys // 128):
        part = slice(i * 128, (i + 1) * 128)
        weight = jnp.exp2(scores[:, part] - peak)
        scores[:, part] = weight
        mass = mass + weight
        moment = moment + weight * grads[:, part]
    mass = jnp.sum(mass, axis=1, keepdims=True)
    moment = jnp.sum(moment, axis=1, keepdims=True)
    centre = jnp.where(mass > 0.0, moment / jnp.where(mass > 0.0, mass, 1.0), 0.0)
    for i in range(keys // size):
        part = slice(i * size, (i + 1) * size)
        weight = scores[:, part]
        low = weight.astype(jnp.bfloat16)
        lean = (weight * (grads[:, part] - centre)).astype(jnp.bfloat16)
        for t in range(tokens):
            weights_ref[t, :heads, part] = low[t * heads : (t + 1) * heads]
            weights_ref[t, heads:, part] = lean[t * heads : (t + 1) * heads]
    column = lax.broadcasted_iota(jnp.int32, (rows, 128), 1)
    table = jnp.where(column == 0, peak, jnp.where(column == 1, mass, jnp.where(column == 2, centre, 0.0)))
    table = jnp.transpose(table)[:8, :]
    for n in range(stats_ref.shape[0]):
        stats_ref[n] = table


def combine(stats):
    top = functools.reduce(jnp.maximum, [s[0] for s in stats])
    shares = [jnp.exp2(s[0] - top) for s in stats]
    mass = functools.reduce(jnp.add, [f * s[1] for f, s in zip(shares, stats)])
    moment = functools.reduce(jnp.add, [f * s[1] * s[2] for f, s in zip(shares, stats)])
    return top, shares, mass, moment / mass


def latent_kernel(heads, offsets, first_ref, head_ref, visible_ref, stats_ref, cache_ref, *refs):
    slots = refs[: len(offsets)]
    out_ref, packed, log_mass, delta_ref, limit_ref, sems = refs[len(offsets) :]
    keys, width = cache_ref.shape
    values = packed.shape[1] - width
    rows = slots[0].shape[0]
    tokens = rows // heads
    total = packed.shape[0]
    step = pl.program_id(0)

    @pl.when(step == 0)
    def _():
        copies = [
            pltpu.make_async_copy(slot, packed.at[pl.ds(j * rows, rows)], sems.at[j])
            for j, slot in enumerate(slots)
        ]
        for copy in copies:
            copy.start()
        token_of = lax.broadcasted_iota(jnp.int32, (1, rows), 1) // heads
        limit = jnp.zeros((1, rows), jnp.int32)
        for t in range(tokens):
            limit = jnp.where(token_of == t, visible_ref[t], limit)
        limit = limit - first_ref[0]
        for j, offset in enumerate(offsets):
            group = head_ref[0] ^ offset
            parts = [stats_ref[c, group] for c in range(stats_ref.shape[0])]
            top, _, mass, delta = combine([(p[0:1], p[1:2], p[2:3]) for p in parts])
            log_mass[:, j * rows : (j + 1) * rows] = top + jnp.log2(mass)
            delta_ref[:, j * rows : (j + 1) * rows] = delta
            limit_ref[:, j * rows : (j + 1) * rows] = limit
        for copy in copies:
            copy.wait()

    block = cache_ref[...]
    span = min(512, total)
    key = lax.broadcasted_iota(jnp.int32, (keys, span), 0) + step * keys
    acc = None
    for r in range(total // span):
        part = slice(r * span, (r + 1) * span)
        cotangent = packed[part, :values]
        rotated = packed[part, values:]
        score = matmul(block, rotated, MINOR) * exp2_scale
        score = jnp.where(key < limit_ref[:, part], score - log_mass[:, part], masked_value)
        prob = jnp.exp2(score)
        grad = matmul(block[:, :values], cotangent, MINOR)
        lean = (prob * (grad - delta_ref[:, part]) * softmax_scale).astype(jnp.bfloat16)
        main = matmul(lean, rotated[:, :values], MAJOR) + matmul(prob.astype(jnp.bfloat16), cotangent, MAJOR)
        side = matmul(lean, rotated[:, values:], MAJOR)
        acc = (main, side) if acc is None else (acc[0] + main, acc[1] + side)
    out_ref[:, :values] = acc[0].astype(jnp.bfloat16)
    out_ref[:, values:] = acc[1].astype(jnp.bfloat16)


def finish_kernel(heads, head_ref, ctx_ref, stats_ref, partial_ref, turn_ref, swap_ref, attention_ref, grad_ref, column):
    shards = partial_ref.shape[0]
    tokens = attention_ref.shape[0]
    values = attention_ref.shape[2]
    rows = stats_ref.shape[3]
    parts = [stats_ref[c, head_ref[0]] for c in range(shards)]
    parts = [(p[0:1], p[1:2], p[2:3]) for p in parts]
    top, shares, mass, delta = combine(parts)
    factors = [f / mass for f in shares]
    shifts = [p[2] - delta for p in parts]
    table = jnp.concatenate(factors + shifts + [jnp.zeros((128 - 2 * shards, rows), jnp.float32)], axis=0)
    column[...] = jnp.transpose(table)
    for t in range(tokens):
        start = pl.multiple_of((ctx_ref[0] * tokens + t) * heads, heads)
        own = column[pl.ds(start, heads), :]
        attended = jnp.zeros((heads, values), jnp.float32)
        rotated = jnp.zeros((heads, grad_ref.shape[2]), jnp.float32)
        for c in range(shards):
            factor = own[:, c : c + 1]
            shift = own[:, shards + c : shards + c + 1]
            first = partial_ref[c, t, :heads, :].astype(jnp.float32)
            second = partial_ref[c, t, heads:, :].astype(jnp.float32)
            attended = attended + factor * first[:, :values]
            rotated = rotated + factor * (second + shift * first)
        attention_ref[t] = attended.astype(jnp.bfloat16)
        rotated = rotated * softmax_scale
        grad_ref[t, :, :values] = rotated[:, :values]
        rope = rotated[:, values:]
        swapped = jnp.dot(rope, swap_ref[...], preferred_element_type=jnp.float32, precision=lax.Precision.HIGHEST)
        grad_ref[t, :, values:] = rope * turn_ref[t, 0:1, :] - swapped * turn_ref[t, 1:2, :]


def whole(space=pltpu.VMEM):
    return pl.BlockSpec(memory_space=space)


def body(query, cache, cotangent, positions, visible, *, shards, groups):
    tokens, heads, width = query.shape
    values = cotangent.shape[2]
    rotary = width - values
    keys = cache.shape[0]
    rows = shards * tokens * heads
    first_key = (lax.axis_index("ctx") * keys).astype(jnp.int32).reshape(1)
    ctx = lax.axis_index("ctx").astype(jnp.int32).reshape(1)
    head = lax.axis_index("head").astype(jnp.int32).reshape(1)
    cos_table, sin_table = rotation_tables(rotary // 2)
    swap = jnp.asarray(swap_matrix(rotary // 2))
    smem, vmem, hbm = whole(pltpu.SMEM), whole(), whole(pl.ANY)

    packed, turn = pl.pallas_call(
        prepare_kernel,
        out_shape=(
            jax.ShapeDtypeStruct((shards, tokens, heads, values + width), jnp.bfloat16),
            jax.ShapeDtypeStruct((tokens, 2, rotary), jnp.float32),
        ),
        in_specs=[smem] + [vmem] * 5,
        out_specs=(vmem, vmem),
        name="prepare",
    )(positions, query, cotangent, jnp.asarray(cos_table), jnp.asarray(sin_table), swap)
    packed = lax.all_to_all(packed, "ctx", 0, 0, tiled=True).reshape(rows, values + width)

    slots, offsets = [packed], [0]
    bit = groups // 2
    while bit:
        pairs = [(h, h ^ bit) for h in range(groups)]
        slots = slots + [lax.ppermute(s, "head", pairs) for s in slots]
        offsets = offsets + [o ^ bit for o in offsets]
        bit //= 2

    chunks = 8
    weights, stats = pl.pallas_call(
        functools.partial(score_kernel, chunks, heads),
        out_shape=(
            jax.ShapeDtypeStruct((shards * tokens, 2 * heads, keys), jnp.bfloat16),
            jax.ShapeDtypeStruct((shards * groups, 8, rows), jnp.float32),
        ),
        in_specs=[smem, smem, vmem, hbm],
        out_specs=(vmem, vmem),
        scratch_shapes=[
            pltpu.VMEM((keys, width), jnp.bfloat16),
            pltpu.VMEM((rows, keys), jnp.float32),
            pltpu.VMEM((rows, keys), jnp.float32),
            pltpu.SemaphoreType.DMA((chunks,)),
        ],
        name="score",
    )(first_key, visible, packed, cache)
    stats = lax.all_to_all(stats, ("ctx", "head"), 0, 0, tiled=True).reshape(shards, groups, 8, rows)

    partial = jnp.einsum("tak,kl->tal", weights, cache, preferred_element_type=jnp.float32).astype(jnp.bfloat16)
    partial = lax.all_to_all(partial, "ctx", 0, 0, tiled=True).reshape(shards, tokens, 2 * heads, width)

    size = 512
    total = rows * groups
    grad_cache = pl.pallas_call(
        functools.partial(latent_kernel, heads, tuple(offsets)),
        out_shape=jax.ShapeDtypeStruct((keys, width), jnp.bfloat16),
        grid=(keys // size,),
        in_specs=[smem, smem, smem, vmem, pl.BlockSpec((size, width), lambda i: (i, 0))] + [hbm] * groups,
        out_specs=pl.BlockSpec((size, width), lambda i: (i, 0)),
        scratch_shapes=[
            pltpu.VMEM((total, values + width), jnp.bfloat16),
            pltpu.VMEM((1, total), jnp.float32),
            pltpu.VMEM((1, total), jnp.float32),
            pltpu.VMEM((1, total), jnp.int32),
            pltpu.SemaphoreType.DMA((groups,)),
        ],
        name="latent",
    )(first_key, head, visible, stats, cache, *slots)

    attention, grad_query = pl.pallas_call(
        functools.partial(finish_kernel, heads),
        out_shape=(
            jax.ShapeDtypeStruct((tokens, heads, values), jnp.bfloat16),
            jax.ShapeDtypeStruct((tokens, heads, width), jnp.float32),
        ),
        in_specs=[smem, smem] + [vmem] * 4,
        out_specs=(vmem, vmem),
        scratch_shapes=[pltpu.VMEM((rows, 128), jnp.float32)],
        name="finish",
    )(head, ctx, stats, partial, turn, swap)
    return attention, grad_query, grad_cache


def solution(mesh):
    shards, groups = mesh.shape["ctx"], mesh.shape["head"]
    placed = (P("ctx", "head", None), P("ctx", None), P("ctx", "head", None), P("ctx"), P())
    return jax.shard_map(
        functools.partial(body, shards=shards, groups=groups),
        mesh=mesh,
        in_specs=placed,
        out_specs=(P("ctx", "head", None), P("ctx", "head", None), P("ctx", None)),
        check_vma=False,
    )
```
